32 devices in a mesh: dp: 8 (over z, y), seq: 4 (over x, core).
Axes of the slice: x: 2, y: 2, z: 4, core: 2. Of those that a mesh axis runs over, the one named last changes fastest.
Arguments:
- patches: bfloat16 [8, 2048, 1024], P('dp', 'seq'), may hold values from -6 to 6
- position_table: bfloat16 [50, 1024], P(None, 'seq'), may hold values from -3 to 3
- qkv_weight: bfloat16 [1024, 3072], P(None, 'seq'), may hold values from -0.1875 to 0.1875
- proj_bias: bfloat16 [3, 1024], P(None, 'seq'), may hold values from -1 to 1
- out_weight: bfloat16 [1024, 1024], P(None, 'seq'), may hold values from -1.5 to 1.5
- up_weight: bfloat16 [1024, 4096], P(None, 'seq'), may hold values from -0.1875 to 0.1875
- up_bias: bfloat16 [4096], P('seq'), may hold values from -1.5 to 1.5
- down_weight: bfloat16 [4096, 1024], P(None, 'seq'), may hold values from -0.09375 to 0.09375
- down_bias: bfloat16 [1024], P('seq'), may hold values from -1.5 to 1.5
- norm_gain: bfloat16 [2, 1024], P(None, 'seq'), may hold values from 0.5 to 1.5
- norm_bias: bfloat16 [2, 1024], P(None, 'seq'), may hold values from -1 to 1
- image_class: int32 [8, 14], P('dp'), may hold values from 0 to 1
- cotangent: bfloat16 [8, 2048, 1024], P('dp', 'seq'), may hold values from -6 to 6
Outputs:
- output: bfloat16 [8, 2048, 1024], P('dp', 'seq')
- input_grad: bfloat16 [8, 2048, 1024], P('dp', 'seq')
- grad_position: float32 [50, 1024], P(None, 'seq')
- grad_qkv: float32 [1024, 3072], P(None, 'seq')
- grad_proj_bias: float32 [3, 1024], P(None, 'seq')
- grad_out_weight: float32 [1024, 1024], P(None, 'seq')
- grad_up: float32 [1024, 4096], P(None, 'seq')
- grad_up_bias: float32 [4096], P('seq')
- grad_down: float32 [4096, 1024], P(None, 'seq')
- grad_down_bias: float32 [1024], P('seq')
- grad_norm_gain: float32 [2, 1024], P(None, 'seq')
- grad_norm_bias: float32 [2, 1024], P(None, 'seq')
The draws below stay inside these ranges and needn't reach their ends.
Inputs may be any that keep to these rules, and one draw needn't show every extreme that they name: `image_class`: 0 marks a 224-pixel image of 50 tokens, 1 a 384-pixel image of 145 tokens; a pack's 14 images lie end to end from its first position, the rest of the pack is padding.
All inputs are finite; a program needn't handle non-finite values.
Results may differ from the reference program's by a relative error of at most 0.014.
Values may be sent and summed in bfloat16 or wider, within the bound.
No kernel may reach another device: no remote copies, remote signals or barrier semaphores. Data moves between devices by JAX's collectives and lax.ppermute only.
A program may use at most 192 MiB of HBM per device.

```python
import math
import jax
import jax.numpy as jnp
import numpy as np
from jax import lax

D = 1024
HEADS = 16
FF = 4096
POS = 50
PACK = 2048
PACKS = 8
IMGS = 14


def plant(entries, own_key, low, largest):
    longest = entries.shape.index(max(entries.shape))
    spots = []
    for shift in (0, 1):
        where = [jax.random.randint(jax.random.fold_in(own_key, axis), (), 0, length) for axis, length in enumerate(entries.shape)]
        where[longest] = (where[longest] + shift) % entries.shape[longest]
        spots.append(tuple(where))
    return entries.at[spots[0]].set(low).at[spots[1]].set(largest)


def block_levels(stream_key, shape, shards, low, top_value):
    def one(dim, parts):
        heights = jax.random.uniform(jax.random.fold_in(jax.random.fold_in(stream_key, 6), dim), (parts,), jnp.float32, low / len(shards), top_value / len(shards))
        return jnp.repeat(jnp.exp(heights), shape[dim] // parts).reshape((-1,) + (1,) * (len(shape) - dim - 1))

    level = one(*shards[0])
    for cut in shards[1:]:
        level = level * one(*cut)
    return level


def gaussian(own_key, extent, spread, limit, shards=(), kind=jnp.bfloat16):
    values = jax.random.normal(own_key, extent, jnp.float32) * spread
    if len(shards) > 0:
        values = block_levels(own_key, extent, shards, -0.22, 0.18) * values
    return jnp.clip(values, min=-limit, max=limit).astype(kind)


def setup_inputs(seed: int = 0) -> dict:
    seeds = jax.random.split(jax.random.key(seed), 14)
    patches = gaussian(seeds[0], (PACKS, PACK, D), 1.0, 6.0, ((0, 8), (1, 4)))
    position_table = gaussian(seeds[1], (POS, D), 0.5, 3.0, ((1, 4),))
    qkv_weight = gaussian(seeds[2], (D, 3 * D), D ** -0.5, 0.1875, ((1, 4),))
    proj_bias = gaussian(seeds[3], (3, D), 0.2, 1.0, ((1, 4),))
    out_weight = gaussian(seeds[4], (D, D), (D // 64) ** -0.5, 1.5, ((1, 4),))
    up_weight = gaussian(seeds[5], (D, FF), D ** -0.5, 0.1875, ((1, 4),))
    up_bias = gaussian(seeds[6], (FF,), 0.3, 1.5, ((0, 4),))
    down_weight = gaussian(seeds[7], (FF, D), FF ** -0.5, 0.09375, ((1, 4),))
    down_bias = gaussian(seeds[8], (D,), 0.3, 1.5, ((0, 4),))
    norm_gain = jnp.clip(1.0 + 0.1 * jax.random.normal(seeds[9], (2, D), jnp.float32), 0.5, 1.5).astype(jnp.bfloat16)
    norm_bias = gaussian(seeds[10], (2, D), 0.2, 1.0, ((1, 4),))
    image_class = plant(jax.random.randint(seeds[11], (PACKS, IMGS), 0, 2), jax.random.fold_in(seeds[11], 1), 0, 1).astype(jnp.int32)
    cotangent = gaussian(seeds[12], (PACKS, PACK, D), 1.0, 6.0, ((0, 8), (1, 4)))
    return dict(patches=patches, position_table=position_table, qkv_weight=qkv_weight, proj_bias=proj_bias, out_weight=out_weight, up_weight=up_weight, up_bias=up_bias, down_weight=down_weight, down_bias=down_bias, norm_gain=norm_gain, norm_bias=norm_bias, image_class=image_class, cotangent=cotangent)


@jax.custom_vjp
def low(v):
    return lax.optimization_barrier(v.astype(jnp.bfloat16)).astype(jnp.float32)

@jax.custom_vjp
def low_back(v):
    return v

def low_keep(v):
    return (low(v), None)

def low_pass(kept, grad):
    return (grad,)

def back_keep(v):
    return (v, None)

def back_low(kept, grad):
    return (low(grad),)
low.defvjp(low_keep, low_pass)
low_back.defvjp(back_keep, back_low)

def interp_matrix():
    matrix = np.zeros((256, 50), np.float32)
    for position in range(50):
        matrix[position, position] = 1.0
    matrix[50, 0] = 1.0
    sources = []
    for target in range(12):
        coordinate = min(max((target + 0.5) * 7.0 / 12.0 - 0.5, 0.0), 6.0)
        lower_cell = math.floor(coordinate)
        upper_cell = min(lower_cell + 1, 6)
        sources.append((lower_cell, upper_cell, coordinate - lower_cell))
    for row_out in range(12):
        for col_out in range(12):
            row_low, row_high, row_frac = sources[row_out]
            col_low, col_high, col_frac = sources[col_out]
            target_row = 51 + 12 * row_out + col_out
            for cell_row, row_weight in ((row_low, 1.0 - row_frac), (row_high, row_frac)):
                for cell_col, col_weight in ((col_low, 1.0 - col_frac), (col_high, col_frac)):
                    matrix[target_row, 1 + 7 * cell_row + cell_col] += row_weight * col_weight
    return jnp.asarray(matrix)

def token_layout(classes, positions):
    lengths = 50 + 95 * classes
    image_ends = jnp.cumsum(lengths)
    finished = (positions[:, None] >= image_ends[None, :]).astype(jnp.int32)
    segment = lax.optimization_barrier(jnp.sum(finished, axis=1))
    offset = positions - lax.optimization_barrier(jnp.sum(finished * lengths[None, :], axis=1))
    slots = jnp.arange(classes.shape[0], dtype=jnp.int32)
    chosen = lax.optimization_barrier(jnp.sum((segment[:, None] == slots[None, :]).astype(jnp.int32) * classes[None, :], axis=1))
    token_valid = segment < classes.shape[0]
    table_row = jnp.where(token_valid, offset + 50 * chosen, -1)
    return (segment, token_valid, table_row)

def layer_norm(hidden, gain, shift):
    centered = hidden - lax.optimization_barrier(jnp.mean(hidden, axis=-1, keepdims=True))
    inverse = lax.rsqrt(lax.optimization_barrier(jnp.mean(centered * centered, axis=-1, keepdims=True)) + 1e-06)
    normed = centered * inverse
    return (normed * gain + shift, normed, inverse)

def pack_forward(weights, interp, patch_pack, class_pack):
    position_table, qkv_weight, proj_bias, out_weight, up_weight, up_bias, down_weight, down_bias, norm_gain, norm_bias = weights
    length, width = patch_pack.shape
    highest = lax.Precision.HIGHEST
    positions = jnp.arange(length, dtype=jnp.int32)
    segment, token_valid, table_row = token_layout(class_pack, positions)
    one_hot = (table_row[:, None] == jnp.arange(256, dtype=jnp.int32)[None, :]).astype(jnp.float32)
    extended = jnp.dot(interp, position_table, precision=highest)
    hidden_in = patch_pack + jnp.dot(one_hot, extended, precision=highest)
    attn_in = low(layer_norm(hidden_in, norm_gain[0], norm_bias[0])[0])
    qkv_shift = jnp.concatenate([proj_bias[0], jnp.zeros((width,), jnp.float32), proj_bias[1]])
    projected = jnp.dot(attn_in, qkv_weight, precision=highest) + qkv_shift
    queries = low_back(low(projected[:, :width])).reshape(length, HEADS, -1)
    keys = low_back(low(projected[:, width:2 * width])).reshape(length, HEADS, -1)
    values = low_back(low(projected[:, 2 * width:])).reshape(length, HEADS, -1)
    head_dim = width // HEADS
    scale = head_dim ** (-0.5)
    scores = low_back(jnp.einsum('shd,khd->hsk', queries, keys, precision=highest) * scale)
    same_image = segment[:, None] == segment[None, :]
    scores = jnp.where(same_image[None], scores, -1000000000.0)
    probs = low(jax.nn.softmax(scores, axis=-1))
    mixed = low_back(low(jnp.einsum('hsk,khd->shd', probs, values, precision=highest).reshape(length, width)))
    hidden_mid = hidden_in + low_back(jnp.dot(mixed, out_weight, precision=highest) + proj_bias[2])
    mlp_in = low(layer_norm(hidden_mid, norm_gain[1], norm_bias[1])[0])
    pre_act = low_back(jnp.dot(mlp_in, up_weight, precision=highest) + up_bias)
    activated = low(jax.nn.gelu(pre_act, approximate=False))
    result = hidden_mid + jnp.dot(activated, down_weight, precision=highest) + down_bias
    return result * token_valid[:, None].astype(jnp.float32)

def reference(patches, position_table, qkv_weight, proj_bias, out_weight, up_weight, up_bias, down_weight, down_bias, norm_gain, norm_bias, image_class, cotangent):
    weights = tuple((member.astype(jnp.float32) for member in (position_table, qkv_weight, proj_bias, out_weight, up_weight, up_bias, down_weight, down_bias, norm_gain, norm_bias)))
    interp = interp_matrix()

    def forward(patch_values, weight_values):

        def one_pack(operands):
            return pack_forward(weight_values, interp, operands[0], operands[1])
        return lax.map(jax.checkpoint(one_pack), (patch_values, image_class))
    output, pullback = jax.vjp(forward, patches.astype(jnp.float32), weights)
    grad_in, grads = pullback(cotangent.astype(jnp.float32))
    return (output.astype(jnp.bfloat16), grad_in.astype(jnp.bfloat16), grads[0], grads[1], grads[2], grads[3], grads[4], grads[5], grads[6], grads[7], grads[8], grads[9])
```

```python
from functools import partial
import math

import jax
import jax.numpy as jnp
import numpy as np
from jax import lax
from jax.sharding import PartitionSpec as P


HEAD_DIM = 64


def with_halo(shard, sides, width):
    for axis, dim in sides:
        count, length = (lax.axis_size(axis), shard.shape[dim])
        up = [(i, (i + 1) % count) for i in range(count - 1)]
        down = [(j, i) for i, j in up]
        last = lax.slice_in_dim(shard, length - width, length, axis=dim)
        first = lax.slice_in_dim(shard, 0, width, axis=dim)
        before = lax.ppermute(last, axis, up)
        after = lax.ppermute(first, axis, down)
        shard = jnp.concatenate([before, shard, after], axis=dim)
    return shard


def shifted(block, axis, distance):
    devices = range(lax.axis_size(axis))
    route = [(i - distance, i) for i in devices if i - distance in devices]
    return lax.ppermute(block, axis, route)


def interp_matrix():
    matrix = np.zeros((256, 50), np.float32)
    for position in range(50):
        matrix[position, position] = 1.0
    matrix[50, 0] = 1.0
    sources = []
    for target in range(12):
        coordinate = min(max((target + 0.5) * 7.0 / 12.0 - 0.5, 0.0), 6.0)
        lower_cell = math.floor(coordinate)
        upper_cell = min(lower_cell + 1, 6)
        sources.append((lower_cell, upper_cell, coordinate - lower_cell))
    for row_out in range(12):
        for col_out in range(12):
            row_low, row_high, row_frac = sources[row_out]
            col_low, col_high, col_frac = sources[col_out]
            target_row = 51 + 12 * row_out + col_out
            for cell_row, row_weight in ((row_low, 1.0 - row_frac), (row_high, row_frac)):
                for cell_col, col_weight in ((col_low, 1.0 - col_frac), (col_high, col_frac)):
                    matrix[target_row, 1 + 7 * cell_row + cell_col] += row_weight * col_weight
    return jnp.asarray(matrix)


def token_layout(classes, positions):
    lengths = 50 + 95 * classes
    image_ends = jnp.cumsum(lengths)
    finished = (positions[:, None] >= image_ends[None, :]).astype(jnp.int32)
    segment = jnp.sum(finished, axis=1)
    offset = positions - jnp.sum(finished * lengths[None, :], axis=1)
    slots = jnp.arange(classes.shape[0], dtype=jnp.int32)
    chosen = jnp.sum(
        (segment[:, None] == slots[None, :]).astype(jnp.int32) * classes[None, :], axis=1
    )
    token_valid = segment < classes.shape[0]
    table_row = jnp.where(token_valid, offset + 50 * chosen, -1)
    return (segment, token_valid, table_row)


def layer_norm(hidden, gain, shift):
    centered = hidden - jnp.mean(hidden, axis=-1, keepdims=True)
    inverse = lax.rsqrt(jnp.mean(centered * centered, axis=-1, keepdims=True) + 1e-06)
    normed = centered * inverse
    return (normed * gain + shift, normed, inverse)


def norm_back(grad_normed, normed, inverse, gain):
    scaled = grad_normed * gain
    return inverse * (
        scaled
        - jnp.mean(scaled, axis=-1, keepdims=True)
        - normed * jnp.mean(scaled * normed, axis=-1, keepdims=True)
    )


def contract_rows(left, right, precision=None):
    return lax.dot_general(
        left,
        right,
        (((0,), (0,)), ((), ())),
        precision=precision,
        preferred_element_type=jnp.float32,
    )


def times_transpose(left, right):
    return lax.dot_general(
        left, right, (((1,), (1,)), ((), ())), preferred_element_type=jnp.float32
    )


def split_groups(matrix):
    return jnp.moveaxis(matrix.reshape(matrix.shape[0], -1, 4 * HEAD_DIM), 1, 0)


def join_groups(stacked):
    return jnp.moveaxis(stacked, 0, 1).reshape(stacked.shape[1], -1)


def group_heads(matrix):
    return matrix.reshape(matrix.shape[0], 4, HEAD_DIM)


def masked_scores(query_heads, key_heads, same_image):
    scores = jnp.einsum(
        "shd,khd->hsk", query_heads, key_heads, preferred_element_type=jnp.float32
    ) * HEAD_DIM ** (-0.5)
    return jnp.where(same_image[None], scores, -1000000000.0)


def attend(operands):
    queries, keys_all, values_all, seg_query, seg_keys = operands
    same_image = seg_query[:, None] == seg_keys[None, :]

    def one_group(group):
        query_part, key_part, value_part = group
        scores = masked_scores(group_heads(query_part), group_heads(key_part), same_image)
        highest_score = jnp.max(scores, axis=-1, keepdims=True)
        expo = jnp.exp(scores - highest_score)
        total = jnp.sum(expo, axis=-1, keepdims=True)
        probs_low = (expo / total).astype(jnp.bfloat16)
        mixed = jnp.einsum(
            "hsk,khd->shd", probs_low, group_heads(value_part), preferred_element_type=jnp.float32
        )
        log_total = (highest_score + jnp.log(total))[:, :, 0]
        return (mixed.reshape(mixed.shape[0], -1).astype(jnp.bfloat16), log_total)

    mixed, log_total = lax.map(
        one_group, (split_groups(queries), split_groups(keys_all), split_groups(values_all))
    )
    return (join_groups(mixed), log_total)


def attend_back(operands):
    queries, keys_all, values_all, seg_query, seg_keys, log_total, grad_mixed = operands
    same_image = seg_query[:, None] == seg_keys[None, :]
    scale = HEAD_DIM ** (-0.5)

    def one_group(group):
        query_part, key_part, value_part, group_total, grad_part = group
        query_heads = group_heads(query_part)
        key_heads = group_heads(key_part)
        grad_heads = group_heads(grad_part)
        scores = masked_scores(query_heads, key_heads, same_image)
        probs = jnp.exp(scores - group_total[:, :, None])
        probs_low = probs.astype(jnp.bfloat16)
        grad_probs = jnp.einsum(
            "shd,khd->hsk", grad_heads, group_heads(value_part), preferred_element_type=jnp.float32
        )
        inner = jnp.sum(probs * grad_probs, axis=-1, keepdims=True)
        grad_scores = (probs * (grad_probs - inner)).astype(jnp.bfloat16)
        grad_query = (
            jnp.einsum("hsk,khd->shd", grad_scores, key_heads, preferred_element_type=jnp.float32)
            * scale
        )
        key_term = (
            jnp.einsum("hsk,shd->khd", grad_scores, query_heads, preferred_element_type=jnp.float32)
            * scale
        )
        value_term = jnp.einsum(
            "hsk,shd->khd", probs_low, grad_heads, preferred_element_type=jnp.float32
        )
        return (
            grad_query.reshape(grad_query.shape[0], -1),
            key_term.reshape(key_term.shape[0], -1),
            value_term.reshape(value_term.shape[0], -1),
        )

    grad_query, key_term, value_term = lax.map(
        one_group,
        (
            split_groups(queries),
            split_groups(keys_all),
            split_groups(values_all),
            log_total,
            split_groups(grad_mixed),
        ),
    )
    return (join_groups(grad_query), join_groups(key_term), join_groups(value_term))


def swap(block, axis, distance):
    return lax.ppermute(block, axis, [(i, i ^ distance) for i in range(lax.axis_size(axis))])


def dp_bit(k):
    return (lax.axis_index("dp") >> k) & 1


def half_of(block, which):
    half = block.shape[0] // 2
    return lax.dynamic_slice_in_dim(block, which * half, half, 0)


def two_halves(mine, other, bit):
    return jnp.concatenate([jnp.where(bit == 0, mine, other), jnp.where(bit == 0, other, mine)], axis=0)


def gather_blocks(shard):
    bit = dp_bit(0)
    first = swap(half_of(shard, bit), "seq", 2)
    second = swap(first, "dp", 1)
    across = two_halves(first, second, bit)
    beside = swap(shard, "seq", 1)
    return [shard, beside, across, swap(across, "seq", 1)]


def pick(matrix, index, width):
    return lax.dynamic_slice_in_dim(matrix, index * width, width, matrix.ndim - 1)


def to_blocks(matrix, own):
    width = matrix.shape[-1] // 4
    return [pick(matrix, own ^ r, width) for r in range(4)]


def from_blocks(blocks, own, axis=-1):
    low = (own & 1) == 0
    pairs = [
        jnp.where(low, blocks[0], blocks[1]),
        jnp.where(low, blocks[1], blocks[0]),
        jnp.where(low, blocks[2], blocks[3]),
        jnp.where(low, blocks[3], blocks[2]),
    ]
    front = own < 2
    return jnp.concatenate(
        [
            jnp.where(front, pairs[0], pairs[2]),
            jnp.where(front, pairs[1], pairs[3]),
            jnp.where(front, pairs[2], pairs[0]),
            jnp.where(front, pairs[3], pairs[1]),
        ],
        axis=axis,
    )


def sum_over_dp(block):
    bits = (lax.axis_size("dp") - 1).bit_length()
    current = block
    for k in range(bits):
        bit = dp_bit(k)
        sent = half_of(current, 1 - bit).astype(jnp.bfloat16)
        current = half_of(current, bit).astype(jnp.float32) + swap(sent, "dp", 1 << k).astype(jnp.float32)
    current = current.astype(jnp.bfloat16)
    for k in reversed(range(bits)):
        current = two_halves(current, swap(current, "dp", 1 << k), dp_bit(k))
    return current


def low(block):
    return block.astype(jnp.bfloat16)


def reduce_blocks(make, send_order=lambda r, block: block):
    third = swap(send_order(1, low(make(3))), "seq", 1)
    first = swap(send_order(1, low(make(1))), "seq", 1)
    second = low(make(2) + third.astype(jnp.float32))
    across = swap(send_order(2, second), "seq", 2)
    total = make(0) + first.astype(jnp.float32) + across.astype(jnp.float32)
    return sum_over_dp(low(total))


def shards(
    patches,
    position_table,
    qkv_weight,
    proj_bias,
    out_weight,
    up_weight,
    up_bias,
    down_weight,
    down_bias,
    norm_gain,
    norm_bias,
    image_class,
    cotangent,
):
    highest = lax.Precision.HIGHEST
    pack_count, rows_here, width = patches.shape
    pack_length = rows_here * lax.axis_size("seq")
    tokens_here = pack_count * rows_here
    reach = 144
    own = lax.axis_index("seq")
    quarter = width // 4
    up_rows = up_bias.shape[0] // quarter
    hidden_block = up_bias.shape[0]
    table_rows = position_table.shape[0]

    small = jnp.concatenate(
        [position_table, proj_bias, down_bias[None], norm_gain, norm_bias, up_bias.reshape(up_rows, quarter)], axis=0
    )
    small_blocks = [small] + [swap(small, "seq", r) for r in (1, 2, 3)]
    wide_rows = small.shape[0] - up_rows
    wide = from_blocks([block[:wide_rows] for block in small_blocks], own)
    full_position = wide[:table_rows]
    bias_rows = wide[table_rows : table_rows + 3].astype(jnp.float32)
    full_down_bias = wide[table_rows + 3].astype(jnp.float32)
    gains = wide[table_rows + 4 : table_rows + 6].astype(jnp.float32)
    shifts = wide[table_rows + 6 : table_rows + 8].astype(jnp.float32)
    up_bias_blocks = [block[wide_rows:].reshape(-1).astype(jnp.float32) for block in small_blocks]

    qkv_blocks = gather_blocks(qkv_weight)
    out_up = gather_blocks(jnp.concatenate([out_weight, up_weight], axis=1))
    full_out = from_blocks([block[:, :quarter] for block in out_up], own)
    up_blocks = [block[:, quarter:] for block in out_up]
    down_rows = down_weight.reshape(4, hidden_block, quarter)
    down_own = jnp.concatenate(
        [lax.dynamic_slice_in_dim(down_rows, own ^ r, 1, 0) for r in range(4)], axis=0
    ).reshape(down_weight.shape)
    down_sent = [block.reshape(4, hidden_block, quarter) for block in gather_blocks(down_own)]
    down_blocks = [
        jnp.concatenate([down_sent[r][j ^ r] for r in range(4)], axis=1) for j in range(4)
    ]

    interp = interp_matrix()
    query_positions = own * rows_here + jnp.arange(rows_here, dtype=jnp.int32)
    seg_query, query_valid, table_row = jax.vmap(
        lambda classes: token_layout(classes, query_positions)
    )(image_class)
    one_hot = (table_row.reshape(-1)[:, None] == jnp.arange(256, dtype=jnp.int32)[None, :]).astype(
        jnp.bfloat16
    )
    extended = jnp.dot(interp, full_position.astype(jnp.float32), precision=highest)
    extended_high = low(extended)
    extended_low = low(extended - extended_high.astype(jnp.float32))
    hidden_in = (
        patches.reshape(tokens_here, width).astype(jnp.float32)
        + jnp.dot(one_hot, extended_high, preferred_element_type=jnp.float32)
        + jnp.dot(one_hot, extended_low, preferred_element_type=jnp.float32)
    )
    attn_float, normed_one, inverse_one = layer_norm(hidden_in, gains[0], shifts[0])
    attn_in = low(attn_float)
    qkv_shift = jnp.concatenate([bias_rows[0], jnp.zeros((width,), jnp.float32), bias_rows[1]])
    shift_blocks = to_blocks(qkv_shift, own)
    projected = from_blocks(
        [
            low(jnp.dot(attn_in, qkv_blocks[r], preferred_element_type=jnp.float32) + shift_blocks[r])
            for r in range(4)
        ],
        own,
    )
    query_packs = projected[:, :width].reshape(pack_count, rows_here, width)
    keys_local = projected[:, width : 2 * width].reshape(pack_count, rows_here, width)
    values_local = projected[:, 2 * width :].reshape(pack_count, rows_here, width)
    padded = with_halo(jnp.stack([keys_local, values_local]), (("seq", 2),), reach)
    keys_all, values_all = (padded[0], padded[1])
    key_positions = (
        own * rows_here
        - reach
        + jnp.arange(rows_here + 2 * reach, dtype=jnp.int32)
    )
    inside = (key_positions >= 0) & (key_positions < pack_length)
    seg_keys = jax.vmap(
        lambda classes: jnp.where(inside, token_layout(classes, key_positions)[0], -1)
    )(image_class)
    mixed, log_total = lax.map(attend, (query_packs, keys_all, values_all, seg_query, seg_keys))
    mixed = mixed.reshape(tokens_here, width)
    hidden_mid = (
        hidden_in + jnp.dot(mixed, full_out, preferred_element_type=jnp.float32) + bias_rows[2]
    )
    mlp_float, normed_two, inverse_two = layer_norm(hidden_mid, gains[1], shifts[1])
    mlp_in = low(mlp_float)
    activated = []
    pulls = []
    for r in range(4):
        pre_act = jnp.dot(mlp_in, up_blocks[r], preferred_element_type=jnp.float32) + up_bias_blocks[r]
        act_float, pull = jax.vjp(partial(jax.nn.gelu, approximate=False), pre_act)
        activated.append(low(act_float))
        pulls.append(pull)

    token_mask = query_valid.reshape(-1, 1).astype(jnp.float32)
    grad_out = cotangent.reshape(tokens_here, width) * token_mask.astype(jnp.bfloat16)
    grad_out_float = grad_out.astype(jnp.float32)
    out_blocks = to_blocks(grad_out, own)

    def rows_for(r, block):
        parts = block.reshape(4, hidden_block, block.shape[1])
        return jnp.concatenate([parts[j ^ r] for j in range(4)], axis=0)

    down_total = reduce_blocks(
        lambda r: jnp.concatenate([contract_rows(activated[j], out_blocks[r]) for j in range(4)], axis=0),
        rows_for,
    )
    down_total = down_total.reshape(4, hidden_block, quarter)
    down_total = jnp.concatenate(
        [lax.dynamic_slice_in_dim(down_total, own ^ j, 1, 0) for j in range(4)], axis=0
    ).reshape(down_weight.shape)
    grad_down_bias = jnp.sum(grad_out_float, axis=0)

    grad_out_cat = jnp.concatenate(out_blocks, axis=1)
    grad_pre = [
        low(pulls[j](times_transpose(grad_out_cat, down_blocks[j]))[0]) for j in range(4)
    ]
    grad_up_bias = [jnp.sum(block.astype(jnp.float32), axis=0) for block in grad_pre]
    grad_mlp_in = sum(times_transpose(grad_pre[j], up_blocks[j]) for j in range(4))
    gain_two = jnp.sum(grad_mlp_in * normed_two, axis=0)
    shift_two = jnp.sum(grad_mlp_in, axis=0)
    grad_mid = grad_out_float + norm_back(grad_mlp_in, normed_two, inverse_two, gains[1])
    grad_branch = low(grad_mid)
    branch_blocks = to_blocks(grad_branch, own)
    out_up_total = reduce_blocks(
        lambda r: jnp.concatenate(
            [contract_rows(mixed, branch_blocks[r]), contract_rows(mlp_in, grad_pre[r])], axis=1
        )
    )
    out_bias_grad = jnp.sum(grad_branch.astype(jnp.float32), axis=0)
    grad_mixed = low(times_transpose(grad_branch, full_out)).reshape(pack_count, rows_here, width)
    grad_queries, key_terms, value_terms = lax.map(
        attend_back, (query_packs, keys_all, values_all, seg_query, seg_keys, log_total, grad_mixed)
    )
    terms = jnp.stack([key_terms, value_terms])
    from_next = shifted(low(terms[:, :, :reach]), "seq", -1).astype(jnp.float32)
    from_prev = shifted(low(terms[:, :, reach + rows_here :]), "seq", 1).astype(jnp.float32)
    middle = terms[:, :, reach : reach + rows_here]
    spare = rows_here - reach
    middle = (
        middle
        + jnp.pad(from_prev, ((0, 0), (0, 0), (0, spare), (0, 0)))
        + jnp.pad(from_next, ((0, 0), (0, 0), (spare, 0), (0, 0)))
    )
    grad_keys, grad_values = (middle[0], middle[1])
    grad_qkv_rows = jnp.concatenate([low(grad_queries), low(grad_keys), low(grad_values)], axis=-1).reshape(
        tokens_here, 3 * width
    )
    row_blocks = to_blocks(grad_qkv_rows, own)
    qkv_total = reduce_blocks(lambda r: contract_rows(attn_in, row_blocks[r]))
    grad_proj_bias = jnp.stack(
        [
            jnp.sum(grad_qkv_rows[:, :width].astype(jnp.float32), axis=0),
            jnp.sum(grad_qkv_rows[:, 2 * width :].astype(jnp.float32), axis=0),
            out_bias_grad,
        ]
    )
    grad_attn_in = sum(times_transpose(row_blocks[r], qkv_blocks[r]) for r in range(4))
    gain_one = jnp.sum(grad_attn_in * normed_one, axis=0)
    shift_one = jnp.sum(grad_attn_in, axis=0)
    grad_in = grad_mid + norm_back(grad_attn_in, normed_one, inverse_one, gains[0])
    input_grad = low(grad_in).reshape(pack_count, rows_here, width)
    row_sums = contract_rows(one_hot, low(grad_in))
    grad_position = contract_rows(interp, row_sums, highest)

    wide_grads = jnp.concatenate(
        [
            grad_position,
            grad_proj_bias,
            grad_down_bias[None],
            jnp.stack([gain_one, gain_two]),
            jnp.stack([shift_one, shift_two]),
        ],
        axis=0,
    )
    small_grads = [
        jnp.concatenate([block, grad_up_bias[r].reshape(up_rows, quarter)], axis=0)
        for r, block in enumerate(to_blocks(wide_grads, own))
    ]
    kept = jnp.stack([small_grads[0], small_grads[2]])
    kept = kept + swap(jnp.stack([small_grads[1], small_grads[3]]), "seq", 1)
    small_total = kept[0] + swap(kept[1], "seq", 2)
    for k in range((lax.axis_size("dp") - 1).bit_length()):
        small_total = small_total + swap(small_total, "dp", 1 << k)

    result = jnp.concatenate(
        [
            sum(
                jnp.dot(activated[j], down_sent[r][j ^ r], preferred_element_type=jnp.float32)
                for j in range(4)
            )
            for r in range(4)
        ],
        axis=1,
    )
    result = from_blocks([result[:, r * quarter : (r + 1) * quarter] for r in range(4)], own)
    output = low((hidden_mid + result + full_down_bias) * token_mask).reshape(pack_count, rows_here, width)

    out_up_total = out_up_total.astype(jnp.float32)
    return (
        output,
        input_grad,
        small_total[:table_rows],
        qkv_total.astype(jnp.float32),
        small_total[table_rows : table_rows + 3],
        out_up_total[:, :quarter],
        out_up_total[:, quarter:],
        small_total[wide_rows:].reshape(-1),
        down_total.astype(jnp.float32),
        small_total[table_rows + 3],
        small_total[table_rows + 4 : table_rows + 6],
        small_total[table_rows + 6 : table_rows + 8],
    )


def solution(mesh):
    in_specs = (
        P("dp", "seq", None),
        P(None, "seq"),
        P(None, "seq"),
        P(None, "seq"),
        P(None, "seq"),
        P(None, "seq"),
        P("seq"),
        P(None, "seq"),
        P("seq"),
        P(None, "seq"),
        P(None, "seq"),
        P("dp", None),
        P("dp", "seq", None),
    )
    out_specs = (
        P("dp", "seq", None),
        P("dp", "seq", None),
        P(None, "seq"),
        P(None, "seq"),
        P(None, "seq"),
        P(None, "seq"),
        P(None, "seq"),
        P("seq"),
        P(None, "seq"),
        P("seq"),
        P(None, "seq"),
        P(None, "seq"),
    )
    return jax.shard_map(shards, mesh=mesh, in_specs=in_specs, out_specs=out_specs, check_vma=False)
```

```python
from functools import partial
import math

import jax
import jax.numpy as jnp
import numpy as np
from jax import lax
from jax.experimental import pallas as pl
from jax.sharding import PartitionSpec as P


HEAD_DIM = 64


def with_halo(shard, sides, width):
    for axis, dim in sides:
        count, length = (lax.axis_size(axis), shard.shape[dim])
        up = [(i, (i + 1) % count) for i in range(count - 1)]
        down = [(j, i) for i, j in up]
        last = lax.slice_in_dim(shard, length - width, length, axis=dim)
        first = lax.slice_in_dim(shard, 0, width, axis=dim)
        before = lax.ppermute(last, axis, up)
        after = lax.ppermute(first, axis, down)
        shard = jnp.concatenate([before, shard, after], axis=dim)
    return shard


def shifted(block, axis, distance):
    devices = range(lax.axis_size(axis))
    route = [(i - distance, i) for i in devices if i - distance in devices]
    return lax.ppermute(block, axis, route)


def interp_matrix():
    matrix = np.zeros((256, 50), np.float32)
    for position in range(50):
        matrix[position, position] = 1.0
    matrix[50, 0] = 1.0
    sources = []
    for target in range(12):
        coordinate = min(max((target + 0.5) * 7.0 / 12.0 - 0.5, 0.0), 6.0)
        lower_cell = math.floor(coordinate)
        upper_cell = min(lower_cell + 1, 6)
        sources.append((lower_cell, upper_cell, coordinate - lower_cell))
    for row_out in range(12):
        for col_out in range(12):
            row_low, row_high, row_frac = sources[row_out]
            col_low, col_high, col_frac = sources[col_out]
            target_row = 51 + 12 * row_out + col_out
            for cell_row, row_weight in ((row_low, 1.0 - row_frac), (row_high, row_frac)):
                for cell_col, col_weight in ((col_low, 1.0 - col_frac), (col_high, col_frac)):
                    matrix[target_row, 1 + 7 * cell_row + cell_col] += row_weight * col_weight
    return jnp.asarray(matrix)


def token_layout(classes, positions):
    lengths = 50 + 95 * classes
    image_ends = jnp.cumsum(lengths)
    finished = (positions[:, None] >= image_ends[None, :]).astype(jnp.int32)
    segment = jnp.sum(finished, axis=1)
    offset = positions - jnp.sum(finished * lengths[None, :], axis=1)
    slots = jnp.arange(classes.shape[0], dtype=jnp.int32)
    chosen = jnp.sum(
        (segment[:, None] == slots[None, :]).astype(jnp.int32) * classes[None, :], axis=1
    )
    token_valid = segment < classes.shape[0]
    table_row = jnp.where(token_valid, offset + 50 * chosen, -1)
    return (segment, token_valid, table_row)


def layer_norm(hidden, gain, shift):
    centered = hidden - jnp.mean(hidden, axis=-1, keepdims=True)
    inverse = lax.rsqrt(jnp.mean(centered * centered, axis=-1, keepdims=True) + 1e-06)
    normed = centered * inverse
    return (normed * gain + shift, normed, inverse)


def norm_back(grad_normed, normed, inverse, gain):
    scaled = grad_normed * gain
    return inverse * (
        scaled
        - jnp.mean(scaled, axis=-1, keepdims=True)
        - normed * jnp.mean(scaled * normed, axis=-1, keepdims=True)
    )


def contract_rows(left, right, precision=None):
    return lax.dot_general(
        left,
        right,
        (((0,), (0,)), ((), ())),
        precision=precision,
        preferred_element_type=jnp.float32,
    )


def times_transpose(left, right):
    return lax.dot_general(
        left, right, (((1,), (1,)), ((), ())), preferred_element_type=jnp.float32
    )


def gelu_parts(pre_act):
    size = jnp.abs(pre_act) * 0.5**0.5
    turn = 1.0 / (1.0 + 0.5 * size)
    poly = jnp.full_like(turn, 0.17087277)
    for coefficient in (-0.82215223, 1.48851587, -1.13520398, 0.27886807, -0.18628806, 0.09678418, 0.37409196, 1.00002368, -1.26551223):
        poly = poly * turn + coefficient
    square = size * size
    tail = 0.5 * turn * jnp.exp(poly - square)
    share = jnp.where(pre_act < 0, tail, 1.0 - tail)
    slope = share + pre_act * jnp.exp(-square) * (2.0 * math.pi) ** -0.5
    return (pre_act * share, slope)


QUERY_BLOCK = 128


def head_lanes():
    return lax.broadcasted_iota(jnp.int32, (1, 2 * HEAD_DIM), 1) < HEAD_DIM


def attend_kernel(reach, width, query_ref, kv_ref, seg_query_ref, seg_key_ref, mixed_ref, total_ref):
    window = QUERY_BLOCK + 2 * reach
    start = pl.multiple_of(pl.program_id(0) * QUERY_BLOCK, QUERY_BLOCK)
    same_image = seg_key_ref[pl.ds(start, window), :] == seg_query_ref[...]
    first_half = head_lanes()
    zero = jnp.zeros((), jnp.bfloat16)
    for pair in range(width // (2 * HEAD_DIM)):
        cols = pl.ds(pair * 2 * HEAD_DIM, 2 * HEAD_DIM)
        query = query_ref[:, cols] * jnp.asarray(HEAD_DIM ** (-0.5), jnp.bfloat16)
        key = kv_ref[pl.ds(start, window), cols]
        value = kv_ref[pl.ds(start, window), pl.ds(width + pair * 2 * HEAD_DIM, 2 * HEAD_DIM)].T
        parts = []
        for side in range(2):
            own_query = jnp.where(first_half == (side == 0), query, zero)
            scores = times_transpose(key, own_query)
            scores = jnp.where(same_image, scores, -1000000000.0)
            highest_score = jnp.max(scores, axis=0, keepdims=True)
            expo = jnp.exp(scores - highest_score)
            total = jnp.sum(expo, axis=0, keepdims=True)
            part = jnp.dot(
                value[side * HEAD_DIM : (side + 1) * HEAD_DIM],
                expo.astype(jnp.bfloat16),
                preferred_element_type=jnp.float32,
            )
            parts.append(part / total)
            total_ref[pl.ds(2 * pair + side, 1), :] = highest_score + jnp.log(total)
        mixed_ref[:, cols] = jnp.concatenate(parts, axis=0).T.astype(jnp.bfloat16)


def attend_back_kernel(
    reach, width, query_ref, kv_ref, seg_query_ref, seg_key_ref, total_ref, grad_ref, grad_query_ref, grad_kv_ref
):
    window = QUERY_BLOCK + 2 * reach
    start = pl.multiple_of(pl.program_id(0) * QUERY_BLOCK, QUERY_BLOCK)

    @pl.when(pl.program_id(0) == 0)
    def _():
        grad_kv_ref[...] = jnp.zeros(grad_kv_ref.shape, jnp.float32)

    same_image = seg_key_ref[pl.ds(start, window), :] == seg_query_ref[...]
    first_half = head_lanes()
    zero = jnp.zeros((), jnp.bfloat16)
    scale = HEAD_DIM ** (-0.5)
    rows = pl.ds(start, window)
    for pair in range(width // (2 * HEAD_DIM)):
        cols = pl.ds(pair * 2 * HEAD_DIM, 2 * HEAD_DIM)
        value_cols = pl.ds(width + pair * 2 * HEAD_DIM, 2 * HEAD_DIM)
        query = query_ref[:, cols] * jnp.asarray(scale, jnp.bfloat16)
        key = kv_ref[rows, cols]
        value = kv_ref[rows, value_cols]
        grad = grad_ref[:, cols]
        key_turned = key.T
        query_parts, probs_parts, scores_parts, own_queries, own_grads = [], [], [], [], []
        for side in range(2):
            own_query = jnp.where(first_half == (side == 0), query, zero)
            own_grad = jnp.where(first_half == (side == 0), grad, zero)
            scores = times_transpose(key, own_query)
            scores = jnp.where(same_image, scores, -1000000000.0)
            probs = jnp.exp(scores - total_ref[pl.ds(2 * pair + side, 1), :])
            grad_probs = times_transpose(value, own_grad)
            inner = jnp.sum(probs * grad_probs, axis=0, keepdims=True)
            grad_scores = (probs * (grad_probs - inner)).astype(jnp.bfloat16)
            query_parts.append(
                jnp.dot(
                    key_turned[side * HEAD_DIM : (side + 1) * HEAD_DIM],
                    grad_scores,
                    preferred_element_type=jnp.float32,
                )
            )
            probs_parts.append(probs.astype(jnp.bfloat16))
            scores_parts.append(grad_scores)
            own_queries.append(own_query)
            own_grads.append(own_grad)
        grad_query_ref[:, cols] = (jnp.concatenate(query_parts, axis=0).T * scale).astype(jnp.bfloat16)
        grad_kv_ref[rows, cols] += jnp.dot(
            jnp.concatenate(scores_parts, axis=1),
            jnp.concatenate(own_queries, axis=0),
            preferred_element_type=jnp.float32,
        )
        grad_kv_ref[rows, value_cols] += jnp.dot(
            jnp.concatenate(probs_parts, axis=1),
            jnp.concatenate(own_grads, axis=0),
            preferred_element_type=jnp.float32,
        )


def attention_specs(projected, kv_all, reach):
    rows_here = projected.shape[0]
    width = kv_all.shape[1] // 2
    query_spec = pl.BlockSpec((QUERY_BLOCK, width), lambda i: (i, 0))
    common = [
        query_spec,
        pl.BlockSpec(kv_all.shape, lambda i: (0, 0)),
        pl.BlockSpec((1, QUERY_BLOCK), lambda i: (0, i)),
        pl.BlockSpec((kv_all.shape[0], 1), lambda i: (0, 0)),
    ]
    total_spec = pl.BlockSpec((width // HEAD_DIM, QUERY_BLOCK), lambda i: (0, i))
    return rows_here, width, query_spec, common, total_spec


def attend_call(projected, kv_all, seg_query, seg_keys, reach):
    rows_here, width, query_spec, common, total_spec = attention_specs(projected, kv_all, reach)
    return pl.pallas_call(
        partial(attend_kernel, reach, width),
        grid=(rows_here // QUERY_BLOCK,),
        in_specs=common,
        out_specs=[query_spec, total_spec],
        out_shape=[
            jax.ShapeDtypeStruct((rows_here, width), jnp.bfloat16),
            jax.ShapeDtypeStruct((width // HEAD_DIM, rows_here), jnp.float32),
        ],
        name="attend",
    )(projected, kv_all, seg_query[None, :], seg_keys[:, None])


def attend_back_call(projected, kv_all, seg_query, seg_keys, log_total, grad_mixed, reach):
    rows_here, width, query_spec, common, total_spec = attention_specs(projected, kv_all, reach)
    return pl.pallas_call(
        partial(attend_back_kernel, reach, width),
        grid=(rows_here // QUERY_BLOCK,),
        in_specs=common + [total_spec, query_spec],
        out_specs=[query_spec, pl.BlockSpec(kv_all.shape, lambda i: (0, 0))],
        out_shape=[
            jax.ShapeDtypeStruct((rows_here, width), jnp.bfloat16),
            jax.ShapeDtypeStruct(kv_all.shape, jnp.float32),
        ],
        name="attend_back",
    )(projected, kv_all, seg_query[None, :], seg_keys[:, None], log_total, grad_mixed)


def swap(block, axis, distance):
    return lax.ppermute(block, axis, [(i, i ^ distance) for i in range(lax.axis_size(axis))])


def dp_bit(k):
    return (lax.axis_index("dp") >> k) & 1


def half_of(block, which):
    half = block.shape[0] // 2
    return lax.dynamic_slice_in_dim(block, which * half, half, 0)


def two_halves(mine, other, bit):
    return jnp.concatenate([jnp.where(bit == 0, mine, other), jnp.where(bit == 0, other, mine)], axis=0)


def gather_blocks(shard, behind=None):
    bit = dp_bit(0)
    half = half_of(shard, bit)
    if behind is not None:
        half, shard, behind = lax.optimization_barrier((half, shard, behind))
    first = swap(half, "seq", 2)
    second = swap(first, "dp", 1)
    across = two_halves(first, second, bit)
    beside = swap(shard, "seq", 1)
    return ([shard, beside, across, swap(across, "seq", 1)], first)


def pick(matrix, index, width):
    return lax.dynamic_slice_in_dim(matrix, index * width, width, matrix.ndim - 1)


def to_blocks(matrix, own):
    width = matrix.shape[-1] // 4
    return [pick(matrix, own ^ r, width) for r in range(4)]


def from_blocks(blocks, own, axis=-1):
    low = (own & 1) == 0
    pairs = [
        jnp.where(low, blocks[0], blocks[1]),
        jnp.where(low, blocks[1], blocks[0]),
        jnp.where(low, blocks[2], blocks[3]),
        jnp.where(low, blocks[3], blocks[2]),
    ]
    front = own < 2
    return jnp.concatenate(
        [
            jnp.where(front, pairs[0], pairs[2]),
            jnp.where(front, pairs[1], pairs[3]),
            jnp.where(front, pairs[2], pairs[0]),
            jnp.where(front, pairs[3], pairs[1]),
        ],
        axis=axis,
    )


def sum_over_dp(block):
    bits = (lax.axis_size("dp") - 1).bit_length()
    current = block
    for k in range(bits):
        bit = dp_bit(k)
        sent = half_of(current, 1 - bit).astype(jnp.bfloat16)
        current = half_of(current, bit).astype(jnp.float32) + swap(sent, "dp", 1 << k).astype(jnp.float32)
    current = current.astype(jnp.bfloat16)
    for k in reversed(range(bits)):
        current = two_halves(current, swap(current, "dp", 1 << k), dp_bit(k))
    return current


def low(block):
    return block.astype(jnp.bfloat16)


def reduce_blocks(make, send_order=lambda r, block: block):
    third = swap(send_order(1, low(make(3))), "seq", 1)
    first = swap(send_order(1, low(make(1))), "seq", 1)
    second = low(make(2) + third.astype(jnp.float32))
    across = swap(send_order(2, second), "seq", 2)
    total = make(0) + first.astype(jnp.float32) + across.astype(jnp.float32)
    return sum_over_dp(low(total))


def shards(
    patches,
    position_table,
    qkv_weight,
    proj_bias,
    out_weight,
    up_weight,
    up_bias,
    down_weight,
    down_bias,
    norm_gain,
    norm_bias,
    image_class,
    cotangent,
):
    highest = lax.Precision.HIGHEST
    pack_count, rows_here, width = patches.shape
    pack_length = rows_here * lax.axis_size("seq")
    tokens_here = pack_count * rows_here
    reach = 144
    own = lax.axis_index("seq")
    quarter = width // 4
    up_rows = up_bias.shape[0] // quarter
    hidden_block = up_bias.shape[0]
    table_rows = position_table.shape[0]

    small = jnp.concatenate(
        [position_table, proj_bias, down_bias[None], norm_gain, norm_bias, up_bias.reshape(up_rows, quarter)], axis=0
    )
    small_blocks = [small] + [swap(small, "seq", r) for r in (1, 2, 3)]
    wide_rows = small.shape[0] - up_rows
    wide = from_blocks([block[:wide_rows] for block in small_blocks], own)
    full_position = wide[:table_rows]
    bias_rows = wide[table_rows : table_rows + 3].astype(jnp.float32)
    full_down_bias = wide[table_rows + 3].astype(jnp.float32)
    gains = wide[table_rows + 4 : table_rows + 6].astype(jnp.float32)
    shifts = wide[table_rows + 6 : table_rows + 8].astype(jnp.float32)
    up_bias_blocks = [block[wide_rows:].reshape(-1).astype(jnp.float32) for block in small_blocks]

    qkv_blocks, sent_first = gather_blocks(qkv_weight)
    out_up, sent_second = gather_blocks(jnp.concatenate([out_weight, up_weight], axis=1), sent_first)
    full_out = from_blocks([block[:, :quarter] for block in out_up], own)
    up_blocks = [block[:, quarter:] for block in out_up]
    down_rows = down_weight.reshape(4, hidden_block, quarter)
    down_own = jnp.concatenate(
        [lax.dynamic_slice_in_dim(down_rows, own ^ r, 1, 0) for r in range(4)], axis=0
    ).reshape(down_weight.shape)
    down_sent = [block.reshape(4, hidden_block, quarter) for block in gather_blocks(down_own, sent_second)[0]]
    down_blocks = [
        jnp.concatenate([down_sent[r][j ^ r] for r in range(4)], axis=1) for j in range(4)
    ]

    interp = interp_matrix()
    query_positions = own * rows_here + jnp.arange(rows_here, dtype=jnp.int32)
    seg_query, query_valid, table_row = jax.vmap(
        lambda classes: token_layout(classes, query_positions)
    )(image_class)
    one_hot = (table_row.reshape(-1)[:, None] == jnp.arange(256, dtype=jnp.int32)[None, :]).astype(
        jnp.bfloat16
    )
    extended = jnp.dot(interp, full_position.astype(jnp.float32), precision=highest)
    extended_high = low(extended)
    extended_low = low(extended - extended_high.astype(jnp.float32))
    hidden_in = (
        patches.reshape(tokens_here, width).astype(jnp.float32)
        + jnp.dot(one_hot, extended_high, preferred_element_type=jnp.float32)
        + jnp.dot(one_hot, extended_low, preferred_element_type=jnp.float32)
    )
    attn_float, normed_one, inverse_one = layer_norm(hidden_in, gains[0], shifts[0])
    attn_in = low(attn_float)
    qkv_shift = jnp.concatenate([bias_rows[0], jnp.zeros((width,), jnp.float32), bias_rows[1]])
    shift_blocks = to_blocks(qkv_shift, own)
    projected = from_blocks(
        [
            low(jnp.dot(attn_in, qkv_blocks[r], preferred_element_type=jnp.float32) + shift_blocks[r])
            for r in range(4)
        ],
        own,
    )
    kv_all = with_halo(projected[:, width:], (("seq", 0),), reach)
    key_positions = (
        own * rows_here
        - reach
        + jnp.arange(rows_here + 2 * reach, dtype=jnp.int32)
    )
    inside = (key_positions >= 0) & (key_positions < pack_length)
    seg_keys = jax.vmap(
        lambda classes: jnp.where(inside, token_layout(classes, key_positions)[0], -1)
    )(image_class)
    mixed, log_total = attend_call(projected, kv_all, seg_query[0], seg_keys[0], reach)
    hidden_mid = (
        hidden_in + jnp.dot(mixed, full_out, preferred_element_type=jnp.float32) + bias_rows[2]
    )
    mlp_float, normed_two, inverse_two = layer_norm(hidden_mid, gains[1], shifts[1])
    mlp_in = low(mlp_float)
    activated = []
    slopes = []
    for r in range(4):
        pre_act = jnp.dot(mlp_in, up_blocks[r], preferred_element_type=jnp.float32) + up_bias_blocks[r]
        act_float, slope = gelu_parts(pre_act)
        activated.append(low(act_float))
        slopes.append(slope)

    token_mask = query_valid.reshape(-1, 1).astype(jnp.float32)
    grad_out = cotangent.reshape(tokens_here, width) * token_mask.astype(jnp.bfloat16)
    grad_out_float = grad_out.astype(jnp.float32)
    out_blocks = to_blocks(grad_out, own)

    def rows_for(r, block):
        parts = block.reshape(4, hidden_block, block.shape[1])
        return jnp.concatenate([parts[j ^ r] for j in range(4)], axis=0)

    down_total = reduce_blocks(
        lambda r: jnp.concatenate([contract_rows(activated[j], out_blocks[r]) for j in range(4)], axis=0),
        rows_for,
    )
    down_total = down_total.reshape(4, hidden_block, quarter)
    down_total = jnp.concatenate(
        [lax.dynamic_slice_in_dim(down_total, own ^ j, 1, 0) for j in range(4)], axis=0
    ).reshape(down_weight.shape)
    grad_down_bias = jnp.sum(grad_out_float, axis=0)

    grad_out_cat = jnp.concatenate(out_blocks, axis=1)
    grad_pre = [
        low(times_transpose(grad_out_cat, down_blocks[j]) * slopes[j]) for j in range(4)
    ]
    grad_up_bias = [jnp.sum(block.astype(jnp.float32), axis=0) for block in grad_pre]
    grad_mlp_in = sum(times_transpose(grad_pre[j], up_blocks[j]) for j in range(4))
    gain_two = jnp.sum(grad_mlp_in * normed_two, axis=0)
    shift_two = jnp.sum(grad_mlp_in, axis=0)
    grad_mid = grad_out_float + norm_back(grad_mlp_in, normed_two, inverse_two, gains[1])
    grad_branch = low(grad_mid)
    branch_blocks = to_blocks(grad_branch, own)
    out_up_total = reduce_blocks(
        lambda r: jnp.concatenate(
            [contract_rows(mixed, branch_blocks[r]), contract_rows(mlp_in, grad_pre[r])], axis=1
        )
    )
    out_bias_grad = jnp.sum(grad_branch.astype(jnp.float32), axis=0)
    grad_mixed = low(times_transpose(grad_branch, full_out))
    grad_queries, terms = attend_back_call(
        projected, kv_all, seg_query[0], seg_keys[0], log_total, grad_mixed, reach
    )
    from_next = shifted(low(terms[:reach]), "seq", -1).astype(jnp.float32)
    from_prev = shifted(low(terms[reach + rows_here :]), "seq", 1).astype(jnp.float32)
    spare = rows_here - reach
    grad_kv = (
        terms[reach : reach + rows_here]
        + jnp.pad(from_prev, ((0, spare), (0, 0)))
        + jnp.pad(from_next, ((spare, 0), (0, 0)))
    )
    grad_qkv_rows = jnp.concatenate([grad_queries, low(grad_kv)], axis=-1)
    row_blocks = to_blocks(grad_qkv_rows, own)
    qkv_total = reduce_blocks(lambda r: contract_rows(attn_in, row_blocks[r]))
    grad_proj_bias = jnp.stack(
        [
            jnp.sum(grad_qkv_rows[:, :width].astype(jnp.float32), axis=0),
            jnp.sum(grad_qkv_rows[:, 2 * width :].astype(jnp.float32), axis=0),
            out_bias_grad,
        ]
    )
    grad_attn_in = sum(times_transpose(row_blocks[r], qkv_blocks[r]) for r in range(4))
    gain_one = jnp.sum(grad_attn_in * normed_one, axis=0)
    shift_one = jnp.sum(grad_attn_in, axis=0)
    grad_in = grad_mid + norm_back(grad_attn_in, normed_one, inverse_one, gains[0])
    input_grad = low(grad_in).reshape(pack_count, rows_here, width)
    row_sums = contract_rows(one_hot, low(grad_in))
    grad_position = contract_rows(interp, row_sums, highest)

    wide_grads = jnp.concatenate(
        [
            grad_position,
            grad_proj_bias,
            grad_down_bias[None],
            jnp.stack([gain_one, gain_two]),
            jnp.stack([shift_one, shift_two]),
        ],
        axis=0,
    )
    small_grads = [
        jnp.concatenate([block, grad_up_bias[r].reshape(up_rows, quarter)], axis=0)
        for r, block in enumerate(to_blocks(wide_grads, own))
    ]
    kept = jnp.stack([small_grads[0], small_grads[2]])
    kept = kept + swap(jnp.stack([small_grads[1], small_grads[3]]), "seq", 1)
    small_total = kept[0] + swap(kept[1], "seq", 2)
    for k in range((lax.axis_size("dp") - 1).bit_length()):
        small_total = small_total + swap(small_total, "dp", 1 << k)

    result = jnp.concatenate(
        [
            sum(
                jnp.dot(activated[j], down_sent[r][j ^ r], preferred_element_type=jnp.float32)
                for j in range(4)
            )
            for r in range(4)
        ],
        axis=1,
    )
    result = from_blocks([result[:, r * quarter : (r + 1) * quarter] for r in range(4)], own)
    output = low((hidden_mid + result + full_down_bias) * token_mask).reshape(pack_count, rows_here, width)

    out_up_total = out_up_total.astype(jnp.float32)
    return (
        output,
        input_grad,
        small_total[:table_rows],
        qkv_total.astype(jnp.float32),
        small_total[table_rows : table_rows + 3],
        out_up_total[:, :quarter],
        out_up_total[:, quarter:],
        small_total[wide_rows:].reshape(-1),
        down_total.astype(jnp.float32),
        small_total[table_rows + 3],
        small_total[table_rows + 4 : table_rows + 6],
        small_total[table_rows + 6 : table_rows + 8],
    )


def solution(mesh):
    in_specs = (
        P("dp", "seq", None),
        P(None, "seq"),
        P(None, "seq"),
        P(None, "seq"),
        P(None, "seq"),
        P(None, "seq"),
        P("seq"),
        P(None, "seq"),
        P("seq"),
        P(None, "seq"),
        P(None, "seq"),
        P("dp", None),
        P("dp", "seq", None),
    )
    out_specs = (
        P("dp", "seq", None),
        P("dp", "seq", None),
        P(None, "seq"),
        P(None, "seq"),
        P(None, "seq"),
        P(None, "seq"),
        P(None, "seq"),
        P("seq"),
        P(None, "seq"),
        P("seq"),
        P(None, "seq"),
        P(None, "seq"),
    )
    return jax.shard_map(shards, mesh=mesh, in_specs=in_specs, out_specs=out_specs, check_vma=False)
```
